32 devices in a mesh: freq: 2 (over y), tile: 8 (over z, x), src: 2 (over core).
Axes of the slice: x: 2, y: 2, z: 4, core: 2. Of those that a mesh axis runs over, the one named last changes fastest.
Arguments:
- green: bfloat16 [2, 4096, 1024], P(None, ('freq', 'tile'), 'src'), parts along dimension 1, may hold values from -0.1875 to 0.1875
- direction: bfloat16 [2, 2048, 1024], P(None, ('freq', 'src')), parts along dimension 1, may hold values from -6 to 6
- partners: int32 [32, 8], P(('freq', 'tile')), parts along dimension 0, may hold values from 0 to 15, as said below
- counts: int32 [32], P(('freq', 'tile')), parts along dimension 0, may hold values from 1 to 8, as said below
Outputs:
- hessian: float32 [2048, 2, 1024], P(('freq', 'tile'), None, 'src'), parts along dimension 0
The draws below stay inside these ranges and needn't reach their ends.
There are 2 independent parts, one for each index of `freq`. The reference program is written for one: setup_inputs(seed, part) draws one part's arguments, and reference() takes and returns one part's arrays. A program takes and returns all parts, laid end to end along the dimension named above; each array names one. Nothing has to cross between parts.
Inputs may be any that keep to these rules, and one draw needn't show every extreme that they name: The entries partners[t, k] of a row are distinct tile indices u with |u // 2 - t // 2| <= 3; only those with k < counts[t] are sampled. `counts`: some tile row has all 8 slots sampled, and some tile row has only one.
All inputs are finite; a program needn't handle non-finite values.
Results may differ from the reference program's by a relative error of at most 0.0016.
Values may be sent and summed in bfloat16 or wider, within the bound.
A program may use at most 64 MiB of HBM per device.

```python
import jax
import jax.numpy as jnp
from jax import lax

TILE = 128
SRC = 1024
TILE_DEV = 2
BAND_DEV = 3
TILES = 16
SENSORS = 2048
KMAX = 8


def pattern_tables(key):
    base_key = jax.random.fold_in(key, 4711)
    key_score, key_left, key_right, key_top, key_bottom = jax.random.split(base_key, 5)
    width = (2 * BAND_DEV + 1) * TILE_DEV
    rows = jnp.arange(TILES, dtype=jnp.int32)
    first = (rows // TILE_DEV - BAND_DEV) * TILE_DEV
    candidate = first[:, None] + jnp.arange(width, dtype=jnp.int32)[None, :]
    inside = (candidate >= 0) & (candidate < TILES)
    score = jax.random.randint(key_score, (TILES, width), 0, 2 ** 20, dtype=jnp.int32) * width
    score = score + jnp.arange(width, dtype=jnp.int32)[None, :]
    score = jnp.where(inside, score, score + 2 ** 26)
    order = jnp.argsort(score, axis=1, stable=True)[:, :KMAX]
    partner_table = jnp.take_along_axis(candidate, order, axis=1).astype(jnp.int32)
    left = jax.random.randint(key_left, (TILES,), 0, KMAX, dtype=jnp.int32)
    right = jax.random.randint(key_right, (TILES,), 0, KMAX, dtype=jnp.int32)
    count_table = jnp.maximum(1, KMAX - left * right // (KMAX - 1))
    top = jax.random.randint(key_top, (), 0, TILES, dtype=jnp.int32)
    bottom = (top + 1 + jax.random.randint(key_bottom, (), 0, TILES - 1, dtype=jnp.int32)) % TILES
    count_table = jnp.where(rows == top, KMAX, count_table)
    count_table = jnp.where(rows == bottom, 1, count_table).astype(jnp.int32)
    return (partner_table, count_table)


def draw_partners(key, part):
    return pattern_tables(key)[0]


def draw_counts(key, part):
    return pattern_tables(key)[1]


def levels(rng, extent, cuts, smallest, largest):
    def one(dim, shards_of):
        draws = jax.random.uniform(jax.random.fold_in(jax.random.fold_in(rng, 6), dim), (shards_of,), jnp.float32, smallest / len(cuts), largest / len(cuts))
        return jnp.repeat(jnp.exp(draws), extent[dim] // shards_of).reshape((-1,) + (1,) * (len(extent) - dim - 1))

    loudness = one(*cuts[0])
    for cut in cuts[1:]:
        loudness = loudness * one(*cut)
    return loudness


def noise(key, dims, scale, reach, cuts=(), kind=jnp.bfloat16):
    loudness = levels(key, dims, cuts, -0.22, 0.18) if cuts else 1.0
    array = jax.random.normal(key, dims, jnp.float32) * scale * loudness
    return jnp.minimum(jnp.maximum(array, -reach), reach).astype(kind)


def setup_inputs(seed: int = 0, part: int = 0) -> dict:
    key_of = jax.random.split(jax.random.key(seed), 5)
    part_splits = jax.random.split(jax.random.fold_in(key_of[4], part), 5)
    green = noise(part_splits[0], (2, SENSORS, SRC), SRC ** -0.5, 0.1875, ((1, 8), (2, 2)))
    direction = noise(part_splits[1], (2, SRC, SRC), 1.0, 6.0, ((1, 2),))
    partners = draw_partners(jax.random.fold_in(jax.random.fold_in(key_of[4], part), 71), part)
    counts = draw_counts(jax.random.fold_in(jax.random.fold_in(key_of[4], part), 71), part)
    return {"green": green, "direction": direction, "partners": partners, "counts": counts}


def reference(green, direction, partners, counts):
    sources = green.shape[2]
    tiles = green.reshape(2, TILES, TILE, sources)
    live = (jnp.arange(KMAX, dtype=jnp.int32)[None, :] < counts[:, None]).astype(jnp.float32)

    def visit(total, index):
        own = lax.dynamic_index_in_dim(tiles, index, 1, keepdims=False)
        image_real = (jnp.dot(own[0], direction[0], preferred_element_type=jnp.float32)
                      - jnp.dot(own[1], direction[1], preferred_element_type=jnp.float32)).astype(jnp.bfloat16)
        image_imag = (jnp.dot(own[0], direction[1], preferred_element_type=jnp.float32)
                      + jnp.dot(own[1], direction[0], preferred_element_type=jnp.float32)).astype(jnp.bfloat16)
        stack = jnp.take(tiles, partners[index].astype(jnp.int32), axis=1).reshape(2, KMAX * TILE, sources)
        mask = jnp.repeat(live[index], TILE)[None, :]
        couple_real = (jnp.dot(image_real, stack[0].T, preferred_element_type=jnp.float32)
                       + jnp.dot(image_imag, stack[1].T, preferred_element_type=jnp.float32))
        couple_imag = (jnp.dot(image_imag, stack[0].T, preferred_element_type=jnp.float32)
                       - jnp.dot(image_real, stack[1].T, preferred_element_type=jnp.float32))
        couple_real = (couple_real * mask).astype(jnp.bfloat16)
        couple_imag = (couple_imag * mask).astype(jnp.bfloat16)
        weight_real = (jnp.dot(couple_real, stack[0], preferred_element_type=jnp.float32)
                       - jnp.dot(couple_imag, stack[1], preferred_element_type=jnp.float32)).astype(jnp.bfloat16)
        weight_imag = (jnp.dot(couple_real, stack[1], preferred_element_type=jnp.float32)
                       + jnp.dot(couple_imag, stack[0], preferred_element_type=jnp.float32)).astype(jnp.bfloat16)
        out_real = (jnp.dot(own[0].T, weight_real, preferred_element_type=jnp.float32)
                    + jnp.dot(own[1].T, weight_imag, preferred_element_type=jnp.float32))
        out_imag = (jnp.dot(own[0].T, weight_imag, preferred_element_type=jnp.float32)
                    - jnp.dot(own[1].T, weight_real, preferred_element_type=jnp.float32))
        return total + jnp.stack([out_real, out_imag], axis=1), None

    start = jnp.zeros((sources, 2, sources), jnp.float32)
    total, _ = lax.scan(visit, start, jnp.arange(TILES, dtype=jnp.int32))
    return total
```

```python
import functools

import jax
import jax.numpy as jnp
from jax import lax
from jax.experimental import pallas as pl
from jax.experimental.pallas import tpu as pltpu
from jax.sharding import PartitionSpec as P

BAND_DEV = 3
PIECES = 4
CHUNKS = 2
OWN, ACROSS, NEAR, BACK, BACK_ACROSS, NEAR_ACROSS, FAR, PAIR, PAIR_ACROSS = range(9)
OFFSETS = (0, 1, 2, -2, -1, 3, -3)
ROUTES = (
    (OWN, ACROSS),
    (OWN, BACK),
    (OWN, NEAR),
    (ACROSS, NEAR_ACROSS),
    (NEAR, BACK_ACROSS),
    (BACK_ACROSS, FAR),
)
F32 = jnp.float32
BF16 = jnp.bfloat16


def dot(left, right, dims):
    return lax.dot_general(left, right, (dims, ((), ())), preferred_element_type=F32)


def kernel(
    count_tile, a_ref, v_ref, mask_ref, out_ref,
    win, vbuf, img, ipart, irecv, cpart, crecv, acc, w, rr, hp, hr,
    load_sem, img_sem, route_send, route_recv, couple_send, couple_recv,
    pair_send, pair_recv, w_send, w_recv, h_send, h_recv,
):
    me = lax.axis_index("tile")
    core = lax.axis_index("src")
    side = lax.rem(me, 2)
    level = me // 2
    levels = count_tile // 2
    step = 1 - 2 * side
    rows, half = win.shape[2], win.shape[3]
    tiles = mask_ref.shape[1]
    out_rows = out_ref.shape[1]
    wide = half // CHUNKS

    def inside(place):
        return (place >= 0) & (place < levels)

    has_near = inside(level + step)
    has_back = inside(level - step)
    has_far = inside(level - 2 * step)
    across = {"tile": me + step}
    forward = {"tile": me + 2 * step}
    backward = {"tile": me - 2 * step}
    partner = {"src": 1 - core}
    targets = (across, forward, backward, backward, across, forward)
    sends = (None, has_near, has_back, has_back, has_near, has_near & has_back)
    arrives = (None, has_back, has_near, has_near, has_back, has_far)

    def guarded(condition, run):
        if condition is None:
            run()
        else:
            pl.when(condition)(run)

    def remote(source, target, send, recv, device):
        return pltpu.make_async_remote_copy(
            src_ref=source, dst_ref=target, send_sem=send, recv_sem=recv,
            device_id=device, device_id_type=pl.DeviceIdType.MESH,
        )

    def piece(slot, index):
        depth = 2 * rows // PIECES
        per = PIECES // 2
        return win.at[slot, index // per, pl.ds((index % per) * depth, depth)]

    def route(number, index):
        source, target = ROUTES[number]
        return remote(
            piece(source, index), piece(target, index),
            route_send.at[number, index], route_recv.at[number, index], targets[number],
        )

    def send_route(number, index):
        guarded(sends[number], lambda: route(number, index).start())

    def arrive(number, index):
        guarded(arrives[number], lambda: route(number, index).wait_recv())

    def to_pair(source, target, number):
        return remote(win.at[source], win.at[target], pair_send.at[number], pair_recv.at[number], partner)

    load_a = pltpu.make_async_copy(a_ref, win.at[OWN], load_sem.at[0])
    load_theirs = pltpu.make_async_copy(
        v_ref.at[:, :, pl.ds(pl.multiple_of((1 - core) * half, half), half)], vbuf.at[0], load_sem.at[1]
    )
    load_mine = pltpu.make_async_copy(
        v_ref.at[:, :, pl.ds(pl.multiple_of(core * half, half), half)], vbuf.at[1], load_sem.at[2]
    )
    load_a.start()
    load_theirs.start()
    load_mine.start()

    barrier = pltpu.get_barrier_semaphore()
    pl.semaphore_signal(barrier, inc=1, device_id=partner, device_id_type=pl.DeviceIdType.MESH)
    pl.semaphore_signal(barrier, inc=1, device_id=across, device_id_type=pl.DeviceIdType.MESH)

    def other_level(number):
        return lax.rem(level + 1 + number, levels)

    @pl.loop(0, levels - 1)
    def _(number):
        pl.semaphore_signal(
            barrier, inc=1, device_id={"tile": other_level(number) * 2 + side},
            device_id_type=pl.DeviceIdType.MESH,
        )

    pl.semaphore_wait(barrier, levels + 1)
    load_a.wait()
    for index in range(PIECES):
        for number in (0, 1, 2):
            send_route(number, index)
    to_pair(OWN, PAIR, 0).start()

    own = win[OWN].reshape(2 * rows, half)

    def images(slot):
        first = dot(own, vbuf[slot, 0], ((1,), (0,)))
        second = dot(own, vbuf[slot, 1], ((1,), (0,)))
        return first[:rows] - second[rows:], second[:rows] + first[rows:]

    load_theirs.wait()
    real, imag = images(0)
    ipart[0] = real
    ipart[1] = imag
    image_copy = remote(ipart, irecv, img_sem.at[0], img_sem.at[1], partner)
    image_copy.start()
    load_mine.wait()
    real, imag = images(1)
    image_copy.wait_recv()
    img[:rows] = (real + irecv[0]).astype(BF16)
    img[rows:] = (imag + irecv[1]).astype(BF16)

    acc[...] = jnp.zeros_like(acc)

    def exists(slot):
        return (
            (slot <= ACROSS)
            | (((slot == NEAR) | (slot == NEAR_ACROSS)) & has_near)
            | (((slot == BACK) | (slot == BACK_ACROSS)) & has_back)
            | ((slot == FAR) & has_far)
        )

    def couple_copy(slot):
        return remote(cpart.at[slot], crecv.at[slot], couple_send.at[slot], couple_recv.at[slot], partner)

    def couple(low, high):
        @pl.loop(low, high)
        def _(slot):
            @pl.when(exists(slot))
            def _():
                block = win[slot].reshape(2 * rows, half)
                prod = dot(img[...], block, ((1,), (1,)))
                cpart[slot, 0] = prod[:rows, :rows] + prod[rows:, rows:]
                cpart[slot, 1] = prod[rows:, :rows] - prod[:rows, rows:]
                couple_copy(slot).start()

    def weigh(low, high):
        @pl.loop(low, high)
        def _(slot):
            @pl.when(exists(slot))
            def _():
                couple_copy(slot).wait_recv()
                live = jnp.concatenate(
                    [jnp.broadcast_to(mask_ref[slot, row], (rows // tiles, rows)) for row in range(tiles)], axis=0
                )
                real = ((cpart[slot, 0] + crecv[slot, 0]) * live).astype(BF16)
                imag = ((cpart[slot, 1] + crecv[slot, 1]) * live).astype(BF16)
                left = jnp.concatenate(
                    [jnp.concatenate([real, -imag], axis=1), jnp.concatenate([imag, real], axis=1)], axis=0
                )
                acc[...] += dot(left, win[slot].reshape(2 * rows, half), ((1,), (0,)))

    def pass_on(index):
        arrive(0, index)
        send_route(3, index)
        arrive(2, index)
        send_route(4, index)

    couple(OWN, ACROSS)
    for index in range(PIECES):
        pass_on(index)
    to_pair(ACROSS, PAIR_ACROSS, 1).start()
    for index in range(PIECES):
        arrive(1, index)
    couple(ACROSS, BACK_ACROSS)
    weigh(OWN, BACK_ACROSS)
    for index in range(PIECES):
        arrive(4, index)
        send_route(5, index)
    for index in range(PIECES):
        arrive(3, index)
    couple(BACK_ACROSS, FAR)
    weigh(BACK_ACROSS, FAR)
    for index in range(PIECES):
        arrive(5, index)
    couple(FAR, FAR + 1)
    weigh(FAR, FAR + 1)

    def w_copy(chunk):
        return remote(w.at[chunk, 0], w.at[chunk, 1], w_send.at[chunk], w_recv.at[chunk], across)

    for chunk in range(CHUNKS):
        w[chunk, 0] = acc[:, chunk * wide : (chunk + 1) * wide].astype(BF16)
        w_copy(chunk).start()
    to_pair(OWN, PAIR, 0).wait_recv()
    to_pair(ACROSS, PAIR_ACROSS, 1).wait_recv()

    span = max(out_rows, 128)

    def fill(chunk, group):
        if span == out_rows:
            column = (2 * group + side) * out_rows
        else:
            column = group * span
        which = column // half
        base = jnp.where(which == core, OWN, PAIR)
        lanes = pl.ds(pl.multiple_of(column - which * half, 128), span)
        total = dot(win[base, :, :, lanes].reshape(2 * rows, span), rr[0], ((0,), (0,)))
        total += dot(win[base + 1, :, :, lanes].reshape(2 * rows, span), rr[1], ((0,), (0,)))
        hp[chunk, pl.ds(pl.multiple_of(column, span), span)] = total.astype(BF16)

    def term(chunk, target, sender):
        first = pl.multiple_of((2 * target + side) * out_rows, out_rows)
        return remote(
            hp.at[chunk, pl.ds(first, out_rows)], hr.at[chunk, sender],
            h_send.at[chunk, target], h_recv.at[chunk, sender], {"tile": 2 * target + side},
        )

    for chunk in range(CHUNKS):
        w_copy(chunk).wait_recv()
        for block in range(2):
            top, low = w[chunk, block, :rows], w[chunk, block, rows:]
            rr[block, :rows] = jnp.concatenate([top, low], axis=1)
            rr[block, rows:] = jnp.concatenate([low, -top], axis=1)
        if span != out_rows:
            @pl.loop(0, hp.shape[1] // span)
            def _(group):
                fill(chunk, group)

        @pl.loop(0, levels - 1)
        def _(number):
            target = other_level(number)
            if span == out_rows:
                fill(chunk, target)
            term(chunk, target, level).start()

        if span == out_rows:
            fill(chunk, level)

    mine = pl.ds(pl.multiple_of((2 * level + side) * out_rows, out_rows), out_rows)
    for chunk in range(CHUNKS):
        def add(number, total):
            sender = other_level(number)
            term(chunk, level, sender).wait_recv()
            return total + hr[chunk, sender].astype(F32)

        total = lax.fori_loop(0, levels - 1, add, hp[chunk, mine].astype(F32))
        out_ref[0, :, chunk * wide : (chunk + 1) * wide] = total[:, :wide]
        out_ref[1, :, chunk * wide : (chunk + 1) * wide] = total[:, wide:]

    for number in range(len(ROUTES)):
        for index in range(PIECES):
            guarded(sends[number], lambda number=number, index=index: route(number, index).wait_send())
    to_pair(OWN, PAIR, 0).wait_send()
    to_pair(ACROSS, PAIR_ACROSS, 1).wait_send()
    image_copy.wait_send()

    @pl.loop(0, FAR + 1)
    def _(slot):
        @pl.when(exists(slot))
        def _():
            couple_copy(slot).wait_send()

    for chunk in range(CHUNKS):
        w_copy(chunk).wait_send()

        @pl.loop(0, levels - 1)
        def _(number):
            term(chunk, other_level(number), level).wait_send()


def shards(count_tile, green, direction, partners, counts):
    tile_dev, kmax = partners.shape
    rows, half = green.shape[1:]
    tile = rows // tile_dev
    sources = direction.shape[2]
    out_rows = sources // count_tile
    levels = count_tile // 2
    wide = half // CHUNKS
    me = lax.axis_index("tile")
    step = 1 - 2 * (me % 2)
    offsets = jnp.array(OFFSETS, jnp.int32) * step
    block_tiles = (me + offsets)[:, None] * tile_dev + jnp.arange(tile_dev, dtype=jnp.int32)[None, :]
    live = jnp.arange(kmax, dtype=jnp.int32)[None, :] < counts[:, None]
    hit = (partners[None, :, None, :] == block_tiles[:, None, :, None]) & live[None, :, None, :]
    mask = jnp.repeat(jnp.any(hit, axis=3).astype(F32), tile, axis=2)[:, :, None, :]
    anywhere = pl.BlockSpec(memory_space=pl.ANY)
    local = pl.BlockSpec(memory_space=pltpu.VMEM)
    dma = pltpu.SemaphoreType.DMA
    out = pl.pallas_call(
        functools.partial(kernel, count_tile),
        out_shape=jax.ShapeDtypeStruct((2, out_rows, half), F32),
        in_specs=[anywhere, anywhere, local],
        out_specs=local,
        scratch_shapes=[
            pltpu.VMEM((9, 2, rows, half), BF16),
            pltpu.VMEM((2, 2, half, half), BF16),
            pltpu.VMEM((2 * rows, half), BF16),
            pltpu.VMEM((2, rows, half), F32),
            pltpu.VMEM((2, rows, half), F32),
            pltpu.VMEM((FAR + 1, 2, rows, rows), F32),
            pltpu.VMEM((FAR + 1, 2, rows, rows), F32),
            pltpu.VMEM((2 * rows, half), F32),
            pltpu.VMEM((CHUNKS, 2, 2 * rows, wide), BF16),
            pltpu.VMEM((2, 2 * rows, 2 * wide), BF16),
            pltpu.VMEM((CHUNKS, sources, 2 * wide), BF16),
            pltpu.VMEM((CHUNKS, levels, out_rows, 2 * wide), BF16),
            dma((3,)),
            dma((2,)),
            dma((len(ROUTES), PIECES)),
            dma((len(ROUTES), PIECES)),
            dma((FAR + 1,)),
            dma((FAR + 1,)),
            dma((2,)),
            dma((2,)),
            dma((CHUNKS,)),
            dma((CHUNKS,)),
            dma((CHUNKS, levels)),
            dma((CHUNKS, levels)),
        ],
        compiler_params=pltpu.CompilerParams(
            collective_id=0, has_side_effects=True, vmem_limit_bytes=56 * 1024 * 1024
        ),
    )(green, direction, mask)
    return jnp.swapaxes(out, 0, 1)


def solution(mesh):
    in_specs = (
        P(None, ("freq", "tile"), "src"),
        P(None, ("freq", "src"), None),
        P(("freq", "tile"), None),
        P(("freq", "tile")),
    )
    out_specs = P(("freq", "tile"), None, "src")
    body = functools.partial(shards, mesh.shape["tile"])
    return jax.shard_map(body, mesh=mesh, in_specs=in_specs, out_specs=out_specs, check_vma=False)
```

```python
import functools

import jax
import jax.numpy as jnp
from jax import lax
from jax.experimental import pallas as pl
from jax.experimental.pallas import tpu as pltpu
from jax.sharding import PartitionSpec as P

BAND_DEV = 3
PIECES = 4
CHUNKS = 4
OWN, ACROSS, NEAR, BACK, BACK_ACROSS, NEAR_ACROSS, FAR, PAIR, PAIR_ACROSS = range(9)
OFFSETS = (0, 1, 2, -2, -1, 3, -3)
ROUTES = (
    (OWN, ACROSS),
    (OWN, BACK),
    (OWN, NEAR),
    (ACROSS, NEAR_ACROSS),
    (NEAR, BACK_ACROSS),
    (BACK_ACROSS, FAR),
)
F32 = jnp.float32
BF16 = jnp.bfloat16


def dot(left, right, dims):
    return lax.dot_general(left, right, (dims, ((), ())), preferred_element_type=F32)


def short_line(out_rows, levels):
    return out_rows % 128 == 0 and levels <= 4


def kernel(
    count_tile, a_ref, v_ref, partners_ref, counts_ref, out_ref,
    table, sampled, win, vbuf, img, ipart, irecv, cpart, crecv, acc, w, turned, rr, hp, hr,
    load_sem, img_sem, route_send, route_recv, couple_send, couple_recv,
    pair_send, pair_recv, w_send, w_recv, h_send, h_recv, o_send,
):
    me = lax.axis_index("tile")
    core = lax.axis_index("src")
    side = lax.rem(me, 2)
    level = me // 2
    levels = count_tile // 2
    step = 1 - 2 * side
    rows, half = win.shape[2], win.shape[3]
    tiles, kmax = table.shape
    out_rows = out_ref.shape[0]
    wide = half // CHUNKS

    def inside(place):
        return (place >= 0) & (place < levels)

    has_near = inside(level + step)
    has_back = inside(level - step)
    has_far = inside(level - 2 * step)
    across = {"tile": me + step}
    forward = {"tile": me + 2 * step}
    backward = {"tile": me - 2 * step}
    partner = {"src": 1 - core}
    targets = (across, forward, backward, backward, across, forward)
    sends = (None, has_near, has_back, has_back, has_near, has_near & has_back)
    arrives = (None, has_back, has_near, has_near, has_back, has_far)

    def guarded(condition, run):
        if condition is None:
            run()
        else:
            pl.when(condition)(run)

    def remote(source, target, send, recv, device):
        return pltpu.make_async_remote_copy(
            src_ref=source, dst_ref=target, send_sem=send, recv_sem=recv,
            device_id=device, device_id_type=pl.DeviceIdType.MESH,
        )

    def piece(slot, index):
        depth = 2 * rows // PIECES
        per = PIECES // 2
        return win.at[slot, index // per, pl.ds((index % per) * depth, depth)]

    def route(number, index):
        source, target = ROUTES[number]
        return remote(
            piece(source, index), piece(target, index),
            route_send.at[number, index], route_recv.at[number, index], targets[number],
        )

    def send_route(number, index):
        guarded(sends[number], lambda: route(number, index).start())

    def arrive(number, index):
        guarded(arrives[number], lambda: route(number, index).wait_recv())

    def to_pair(source, target, number):
        return remote(win.at[source], win.at[target], pair_send.at[number], pair_recv.at[number], partner)

    load_a = pltpu.make_async_copy(a_ref, win.at[OWN], load_sem.at[0])
    load_theirs = pltpu.make_async_copy(
        v_ref.at[:, :, pl.ds(pl.multiple_of((1 - core) * half, half), half)], vbuf.at[0], load_sem.at[1]
    )
    load_mine = pltpu.make_async_copy(
        v_ref.at[:, :, pl.ds(pl.multiple_of(core * half, half), half)], vbuf.at[1], load_sem.at[2]
    )
    load_table = pltpu.make_async_copy(partners_ref, table, load_sem.at[3])
    load_counts = pltpu.make_async_copy(counts_ref, sampled, load_sem.at[4])
    load_a.start()
    load_table.start()
    load_counts.start()
    load_theirs.start()
    load_mine.start()

    barrier = pltpu.get_barrier_semaphore()
    pl.semaphore_signal(barrier, inc=1, device_id=partner, device_id_type=pl.DeviceIdType.MESH)
    pl.semaphore_signal(barrier, inc=1, device_id=across, device_id_type=pl.DeviceIdType.MESH)

    def other_level(number):
        return lax.rem(level + 1 + number, levels)

    @pl.loop(0, levels - 1)
    def _(number):
        pl.semaphore_signal(
            barrier, inc=1, device_id={"tile": other_level(number) * 2 + side},
            device_id_type=pl.DeviceIdType.MESH,
        )

    pl.semaphore_wait(barrier, levels + 1)
    load_a.wait()
    for index in range(PIECES):
        for number in (0, 1, 2):
            send_route(number, index)
    to_pair(OWN, PAIR, 0).start()

    own = win[OWN].reshape(2 * rows, half)

    def images(slot):
        first = dot(own, vbuf[slot, 0], ((1,), (0,)))
        second = dot(own, vbuf[slot, 1], ((1,), (0,)))
        return first[:rows] - second[rows:], second[:rows] + first[rows:]

    load_theirs.wait()
    real, imag = images(0)
    ipart[0] = real
    ipart[1] = imag
    image_copy = remote(ipart, irecv, img_sem.at[0], img_sem.at[1], partner)
    image_copy.start()
    load_mine.wait()
    real, imag = images(1)
    image_copy.wait_recv()
    img[:rows] = (real + irecv[0]).astype(BF16)
    img[rows:] = (imag + irecv[1]).astype(BF16)

    load_table.wait()
    load_counts.wait()
    acc[...] = jnp.zeros_like(acc)

    def exists(slot):
        return (
            (slot <= ACROSS)
            | (((slot == NEAR) | (slot == NEAR_ACROSS)) & has_near)
            | (((slot == BACK) | (slot == BACK_ACROSS)) & has_back)
            | ((slot == FAR) & has_far)
        )

    def sample(slot):
        offset = 0
        for index, value in enumerate(OFFSETS):
            offset = jnp.where(slot == index, value, offset)
        first = (me + offset * step) * tiles
        tile = rows // tiles
        bands = []
        for row in range(tiles):
            blocks = []
            for column in range(tiles):
                hit = False
                for k in range(kmax):
                    hit = hit | ((table[row, k] == first + column) & (k < sampled[row]))
                blocks.append(jnp.full((tile, tile), jnp.where(hit, 1.0, 0.0), F32))
            bands.append(jnp.concatenate(blocks, axis=1))
        return jnp.concatenate(bands, axis=0)

    def couple_copy(slot):
        return remote(cpart.at[slot], crecv.at[slot], couple_send.at[slot], couple_recv.at[slot], partner)

    def couple(low, high):
        @pl.loop(low, high)
        def _(slot):
            @pl.when(exists(slot))
            def _():
                block = win[slot].reshape(2 * rows, half)
                prod = dot(img[...], block, ((1,), (1,)))
                cpart[slot, 0] = prod[:rows, :rows] + prod[rows:, rows:]
                cpart[slot, 1] = prod[rows:, :rows] - prod[:rows, rows:]
                couple_copy(slot).start()

    def weigh(low, high):
        @pl.loop(low, high)
        def _(slot):
            @pl.when(exists(slot))
            def _():
                couple_copy(slot).wait_recv()
                live = sample(slot)
                real = ((cpart[slot, 0] + crecv[slot, 0]) * live).astype(BF16)
                imag = ((cpart[slot, 1] + crecv[slot, 1]) * live).astype(BF16)
                left = jnp.concatenate(
                    [jnp.concatenate([real, -imag], axis=1), jnp.concatenate([imag, real], axis=1)], axis=0
                )
                acc[...] += dot(left, win[slot].reshape(2 * rows, half), ((1,), (0,)))

    def pass_on(index):
        arrive(0, index)
        send_route(3, index)
        arrive(2, index)
        send_route(4, index)

    couple(OWN, ACROSS)
    for index in range(PIECES):
        pass_on(index)
    to_pair(ACROSS, PAIR_ACROSS, 1).start()
    for index in range(PIECES):
        arrive(1, index)
    span = max(out_rows, 128)

    def turn_over():
        to_pair(OWN, PAIR, 0).wait_recv()
        to_pair(ACROSS, PAIR_ACROSS, 1).wait_recv()

        @pl.loop(0, turned.shape[0])
        def _(group):
            column = (2 * group + side) * out_rows if span == out_rows else group * span
            which = column // half
            base = jnp.where(which == core, OWN, PAIR)
            lanes = pl.ds(pl.multiple_of(column - which * half, 128), span)
            for block in range(2):
                turned[group, :, block * 2 * rows : (block + 1) * 2 * rows] = (
                    win[base + block, :, :, lanes].reshape(2 * rows, span).T
                )

    jobs = (
        lambda: couple(ACROSS, BACK_ACROSS),
        lambda: weigh(OWN, NEAR),
        lambda: weigh(NEAR, BACK_ACROSS),
        turn_over,
    )
    for index in range(PIECES):
        for job in jobs[index * len(jobs) // PIECES : (index + 1) * len(jobs) // PIECES]:
            job()
        arrive(4, index)
        send_route(5, index)
    for index in range(PIECES):
        arrive(3, index)
    couple(BACK_ACROSS, FAR)
    for index in range(PIECES):
        arrive(5, index)
    couple(FAR, FAR + 1)
    weigh(BACK_ACROSS, FAR + 1)

    def w_copy(chunk):
        return remote(w.at[chunk, 0], w.at[chunk, 1], w_send.at[chunk], w_recv.at[chunk], across)

    for chunk in range(CHUNKS):
        w[chunk, 0] = acc[:, chunk * wide : (chunk + 1) * wide].astype(BF16)
        w_copy(chunk).start()
    def partial(chunk, group):
        return dot(turned[group], rr[chunk], ((1,), (0,)))

    def rows_of(target):
        return pl.multiple_of((2 * target + side) * out_rows, out_rows)

    def prepare(chunk):
        w_copy(chunk).wait_recv()
        for block in range(2):
            top, low = w[chunk, block, :rows], w[chunk, block, rows:]
            first = 2 * rows * block
            rr[chunk, first : first + rows] = jnp.concatenate([top, low], axis=1)
            rr[chunk, first + rows : first + 2 * rows] = jnp.concatenate([low, -top], axis=1)

    def put(chunk, total, more=False):
        for part in range(2):
            for index in range(wide // 128):
                place = 2 * (chunk * wide // 128 + index) + part
                first = part * wide + index * 128
                value = total[:, first : first + 128]
                out_ref[:, place] = out_ref[:, place] + value if more else value

    def term(chunk, lane, slot, target, level_to):
        return remote(
            hp.at[chunk, pl.ds(rows_of(target), out_rows)], hr.at[chunk, lane, slot],
            h_send.at[chunk, target], h_recv.at[chunk, lane, slot], {"tile": 2 * level_to + side},
        )

    def onward(chunk, lane, target):
        return remote(
            hr.at[chunk, lane, target], hr.at[chunk, lane, target],
            o_send.at[chunk], h_recv.at[chunk, lane, target], {"tile": 2 * target + side},
        )

    if short_line(out_rows, levels):
        def flow(turn, first):
            lane = jnp.where(2 * level < levels, 1 - first, first)
            depth = jnp.where(lane == 0, level, levels - 1 - level)
            chunk = turn - jnp.maximum(depth - 1, 0)

            @pl.when((chunk >= 0) & (chunk < CHUNKS))
            def _():
                @pl.loop(0, levels - 1 - depth - jnp.where(depth == 0, 1, 0))
                def _(number):
                    target = jnp.where(lane == 0, levels - 1 - number, number)
                    total = partial(chunk, target)
                    passing = term(chunk, lane, target, target, level + 1 - 2 * lane)
                    place = pl.ds(rows_of(target), out_rows)

                    @pl.when(depth == 0)
                    def _():
                        hp[chunk, place] = total.astype(BF16)

                    @pl.when(depth == 1)
                    def _():
                        passing.wait_recv()
                        hp[chunk, place] = (total + hr[chunk, lane, target].astype(F32)).astype(BF16)

                    @pl.when(depth <= 1)
                    def _():
                        passing.start()

                    @pl.when(depth > 1)
                    def _():
                        passing.wait_recv()
                        onward(chunk, lane, target).start()
                        hp[chunk, place] = total.astype(BF16)
                        term(chunk, lane, levels, target, target).start()

        @pl.loop(0, CHUNKS + max(levels - 3, 0))
        def _(turn):
            @pl.when(turn < CHUNKS)
            def _():
                prepare(turn)

            flow(turn, 0)
            flow(turn, 1)

        @pl.when((level == 0) | (level == levels - 1))
        def _():
            lane = jnp.where(level == 0, 0, 1)
            target = level + 1 - 2 * lane

            @pl.loop(0, CHUNKS)
            def _(chunk):
                hp[chunk, pl.ds(rows_of(target), out_rows)] = partial(chunk, target).astype(BF16)
                term(chunk, lane, target, target, target).start()

        for chunk in range(CHUNKS):
            put(chunk, partial(chunk, level))
        for chunk in range(CHUNKS):
            before = level, levels - 1 - level
            for lane, slot, there in (
                (0, level, before[0] > 0), (1, level, before[1] > 0),
                (0, levels, before[0] > 2), (1, levels, before[1] > 2),
            ):
                @pl.when(there)
                def _(chunk=chunk, lane=lane, slot=slot):
                    term(chunk, lane, slot, level, level).wait_recv()
                    total = hr[chunk, lane, slot].astype(F32)
                    put(chunk, total, True)
    else:
        for chunk in range(CHUNKS):
            prepare(chunk)
            if span != out_rows:
                @pl.loop(0, hp.shape[1] // span)
                def _(group):
                    column = pl.multiple_of(group * span, span)
                    hp[chunk, pl.ds(column, span)] = partial(chunk, group).astype(BF16)

            @pl.loop(0, levels - 1)
            def _(number):
                target = other_level(number)
                if span == out_rows:
                    hp[chunk, pl.ds(rows_of(target), out_rows)] = partial(chunk, target).astype(BF16)
                term(chunk, 0, level, target, target).start()

            if span == out_rows:
                hp[chunk, pl.ds(rows_of(level), out_rows)] = partial(chunk, level).astype(BF16)

        for chunk in range(CHUNKS):
            def add(number, total):
                sender = other_level(number)
                term(chunk, 0, sender, level, sender).wait_recv()
                return total + hr[chunk, 0, sender].astype(F32)

            put(chunk, lax.fori_loop(0, levels - 1, add, hp[chunk, pl.ds(rows_of(level), out_rows)].astype(F32)))

    for number in range(len(ROUTES)):
        for index in range(PIECES):
            guarded(sends[number], lambda number=number, index=index: route(number, index).wait_send())
    to_pair(OWN, PAIR, 0).wait_send()
    to_pair(ACROSS, PAIR_ACROSS, 1).wait_send()
    image_copy.wait_send()

    @pl.loop(0, FAR + 1)
    def _(slot):
        @pl.when(exists(slot))
        def _():
            couple_copy(slot).wait_send()

    for chunk in range(CHUNKS):
        w_copy(chunk).wait_send()

        @pl.loop(0, levels - 1)
        def _(number):
            target = other_level(number)
            term(chunk, 0, target, target, target).wait_send()

        if short_line(out_rows, levels) and levels > 3:
            @pl.when((level == 2) | (levels - 1 - level == 2))
            def _(chunk=chunk):
                onward(chunk, 0, 0).wait_send()


def shards(count_tile, green, direction, partners, counts):
    tile_dev, kmax = partners.shape
    rows, half = green.shape[1:]
    sources = direction.shape[2]
    out_rows = sources // count_tile
    levels = count_tile // 2
    wide = half // CHUNKS
    lanes = 2 if short_line(out_rows, levels) else 1
    anywhere = pl.BlockSpec(memory_space=pl.ANY)
    local = pl.BlockSpec(memory_space=pltpu.VMEM)
    dma = pltpu.SemaphoreType.DMA
    out = pl.pallas_call(
        functools.partial(kernel, count_tile),
        out_shape=jax.ShapeDtypeStruct((out_rows, half // 64, 128), F32),
        in_specs=[anywhere] * 4,
        out_specs=local,
        scratch_shapes=[
            pltpu.SMEM((tile_dev, kmax), jnp.int32),
            pltpu.SMEM((tile_dev,), jnp.int32),
            pltpu.VMEM((9, 2, rows, half), BF16),
            pltpu.VMEM((2, 2, half, half), BF16),
            pltpu.VMEM((2 * rows, half), BF16),
            pltpu.VMEM((2, rows, half), F32),
            pltpu.VMEM((2, rows, half), F32),
            pltpu.VMEM((FAR + 1, 2, rows, rows), F32),
            pltpu.VMEM((FAR + 1, 2, rows, rows), F32),
            pltpu.VMEM((2 * rows, half), F32),
            pltpu.VMEM((CHUNKS, 2, 2 * rows, wide), BF16),
            pltpu.VMEM((levels if out_rows >= 128 else sources // 128, max(out_rows, 128), 4 * rows), BF16),
            pltpu.VMEM((CHUNKS, 4 * rows, 2 * wide), BF16),
            pltpu.VMEM((CHUNKS, sources, 2 * wide), BF16),
            pltpu.VMEM((CHUNKS, lanes, levels + 1, out_rows, 2 * wide), BF16),
            dma((5,)),
            dma((2,)),
            dma((len(ROUTES), PIECES)),
            dma((len(ROUTES), PIECES)),
            dma((FAR + 1,)),
            dma((FAR + 1,)),
            dma((2,)),
            dma((2,)),
            dma((CHUNKS,)),
            dma((CHUNKS,)),
            dma((CHUNKS, levels)),
            dma((CHUNKS, lanes, levels + 1)),
            dma((CHUNKS,)),
        ],
        compiler_params=pltpu.CompilerParams(
            collective_id=0, has_side_effects=True, vmem_limit_bytes=56 * 1024 * 1024
        ),
    )(green, direction, partners, counts)
    out = out.reshape(out_rows, half // 128, 2, 128)
    return jnp.swapaxes(out, 1, 2).reshape(out_rows, 2, half)


def solution(mesh):
    in_specs = (
        P(None, ("freq", "tile"), "src"),
        P(None, ("freq", "src"), None),
        P(("freq", "tile"), None),
        P(("freq", "tile")),
    )
    out_specs = P(("freq", "tile"), None, "src")
    body = functools.partial(shards, mesh.shape["tile"])
    return jax.shard_map(body, mesh=mesh, in_specs=in_specs, out_specs=out_specs, check_vma=False)
```

```python
import functools

import jax
import jax.numpy as jnp
from jax import lax
from jax.experimental import pallas as pl
from jax.experimental.pallas import tpu as pltpu
from jax.sharding import PartitionSpec as P

BAND_DEV = 3
PIECES = 8
CHUNKS = 4
OWN, ACROSS, NEAR, BACK, BACK_ACROSS, NEAR_ACROSS, FAR, PAIR, PAIR_ACROSS = range(9)
OFFSETS = (0, 1, 2, -2, -1, 3, -3)
ROUTES = (
    (OWN, ACROSS),
    (OWN, BACK),
    (OWN, NEAR),
    (ACROSS, NEAR_ACROSS),
    (NEAR, BACK_ACROSS),
    (BACK_ACROSS, FAR),
)
F32 = jnp.float32
BF16 = jnp.bfloat16


def dot(left, right, dims):
    return lax.dot_general(left, right, (dims, ((), ())), preferred_element_type=F32)


def short_line(out_rows, levels):
    return out_rows % 128 == 0 and levels <= 4


def kernel(
    count_tile, a_ref, v_ref, partners_ref, counts_ref, out_ref,
    table, sampled, win, vbuf, img, ipart, irecv, cpart, crecv, acc, w, turned, rr, hp, hr,
    load_sem, img_sem, route_send, route_recv, couple_send, couple_recv,
    pair_send, pair_recv, w_send, w_recv, h_send, h_recv, o_send,
):
    me = lax.axis_index("tile")
    core = lax.axis_index("src")
    side = lax.rem(me, 2)
    level = me // 2
    levels = count_tile // 2
    step = 1 - 2 * side
    rows, half = win.shape[2], win.shape[3]
    tiles, kmax = table.shape
    out_rows = out_ref.shape[0]
    wide = half // CHUNKS

    def inside(place):
        return (place >= 0) & (place < levels)

    has_near = inside(level + step)
    has_back = inside(level - step)
    has_far = inside(level - 2 * step)
    across = {"tile": me + step}
    forward = {"tile": me + 2 * step}
    backward = {"tile": me - 2 * step}
    partner = {"src": 1 - core}
    targets = (across, forward, backward, backward, across, forward)
    sends = (None, has_near, has_back, has_back, has_near, has_near & has_back)
    arrives = (None, has_back, has_near, has_near, has_back, has_far)

    def guarded(condition, run):
        if condition is None:
            run()
        else:
            pl.when(condition)(run)

    def remote(source, target, send, recv, device):
        return pltpu.make_async_remote_copy(
            src_ref=source, dst_ref=target, send_sem=send, recv_sem=recv,
            device_id=device, device_id_type=pl.DeviceIdType.MESH,
        )

    def piece(slot, index):
        depth = 2 * rows // PIECES
        per = PIECES // 2
        return win.at[slot, index // per, pl.ds((index % per) * depth, depth)]

    def route(number, index):
        source, target = ROUTES[number]
        return remote(
            piece(source, index), piece(target, index),
            route_send.at[number, index], route_recv.at[number, index], targets[number],
        )

    def send_route(number, index):
        guarded(sends[number], lambda: route(number, index).start())

    def arrive(number, index):
        guarded(arrives[number], lambda: route(number, index).wait_recv())

    def to_pair(source, target, number):
        return remote(win.at[source], win.at[target], pair_send.at[number], pair_recv.at[number], partner)

    load_a = pltpu.make_async_copy(a_ref, win.at[OWN], load_sem.at[0])
    load_theirs = pltpu.make_async_copy(
        v_ref.at[:, :, pl.ds(pl.multiple_of((1 - core) * half, half), half)], vbuf.at[0], load_sem.at[1]
    )
    load_mine = pltpu.make_async_copy(
        v_ref.at[:, :, pl.ds(pl.multiple_of(core * half, half), half)], vbuf.at[1], load_sem.at[2]
    )
    load_table = pltpu.make_async_copy(partners_ref, table, load_sem.at[3])
    load_counts = pltpu.make_async_copy(counts_ref, sampled, load_sem.at[4])
    load_a.start()
    load_table.start()
    load_counts.start()
    load_theirs.start()
    load_mine.start()

    barrier = pltpu.get_barrier_semaphore()
    pl.semaphore_signal(barrier, inc=1, device_id=partner, device_id_type=pl.DeviceIdType.MESH)
    pl.semaphore_signal(barrier, inc=1, device_id=across, device_id_type=pl.DeviceIdType.MESH)

    def other_level(number):
        return lax.rem(level + 1 + number, levels)

    @pl.loop(0, levels - 1)
    def _(number):
        pl.semaphore_signal(
            barrier, inc=1, device_id={"tile": other_level(number) * 2 + side},
            device_id_type=pl.DeviceIdType.MESH,
        )

    pl.semaphore_wait(barrier, levels + 1)
    load_a.wait()
    for index in range(PIECES):
        for number in (0, 1, 2):
            send_route(number, index)
    to_pair(OWN, PAIR, 0).start()

    own = win[OWN].reshape(2 * rows, half)

    def images(slot):
        first = dot(own, vbuf[slot, 0], ((1,), (0,)))
        second = dot(own, vbuf[slot, 1], ((1,), (0,)))
        return first[:rows] - second[rows:], second[:rows] + first[rows:]

    load_theirs.wait()
    real, imag = images(0)
    ipart[0] = real
    ipart[1] = imag
    image_copy = remote(ipart, irecv, img_sem.at[0], img_sem.at[1], partner)
    image_copy.start()
    load_mine.wait()
    real, imag = images(1)
    image_copy.wait_recv()
    img[:rows] = (real + irecv[0]).astype(BF16)
    img[rows:] = (imag + irecv[1]).astype(BF16)

    load_table.wait()
    load_counts.wait()
    acc[...] = jnp.zeros_like(acc)

    def exists(slot):
        return (
            (slot <= ACROSS)
            | (((slot == NEAR) | (slot == NEAR_ACROSS)) & has_near)
            | (((slot == BACK) | (slot == BACK_ACROSS)) & has_back)
            | ((slot == FAR) & has_far)
        )

    def sample(slot):
        offset = 0
        for index, value in enumerate(OFFSETS):
            offset = jnp.where(slot == index, value, offset)
        first = (me + offset * step) * tiles
        tile = rows // tiles
        bands = []
        for row in range(tiles):
            blocks = []
            for column in range(tiles):
                hit = False
                for k in range(kmax):
                    hit = hit | ((table[row, k] == first + column) & (k < sampled[row]))
                blocks.append(jnp.full((tile, tile), jnp.where(hit, 1.0, 0.0), F32))
            bands.append(jnp.concatenate(blocks, axis=1))
        return jnp.concatenate(bands, axis=0)

    def couple_copy(slot):
        return remote(cpart.at[slot], crecv.at[slot], couple_send.at[slot], couple_recv.at[slot], partner)

    def couple(low, high):
        @pl.loop(low, high)
        def _(slot):
            @pl.when(exists(slot))
            def _():
                block = win[slot].reshape(2 * rows, half)
                prod = dot(img[...], block, ((1,), (1,)))
                cpart[slot, 0] = prod[:rows, :rows] + prod[rows:, rows:]
                cpart[slot, 1] = prod[rows:, :rows] - prod[:rows, rows:]
                couple_copy(slot).start()

    def weigh(low, high):
        @pl.loop(low, high)
        def _(slot):
            @pl.when(exists(slot))
            def _():
                couple_copy(slot).wait_recv()
                live = sample(slot)
                real = ((cpart[slot, 0] + crecv[slot, 0]) * live).astype(BF16)
                imag = ((cpart[slot, 1] + crecv[slot, 1]) * live).astype(BF16)
                left = jnp.concatenate(
                    [jnp.concatenate([real, -imag], axis=1), jnp.concatenate([imag, real], axis=1)], axis=0
                )
                acc[...] += dot(left, win[slot].reshape(2 * rows, half), ((1,), (0,)))

    def pass_on(index):
        arrive(0, index)
        send_route(3, index)
        arrive(2, index)
        send_route(4, index)

    couple(OWN, ACROSS)
    for index in range(PIECES):
        pass_on(index)
    to_pair(ACROSS, PAIR_ACROSS, 1).start()
    for index in range(PIECES):
        arrive(1, index)
    span = max(out_rows, 128)

    def turn_over():
        to_pair(OWN, PAIR, 0).wait_recv()
        to_pair(ACROSS, PAIR_ACROSS, 1).wait_recv()

        @pl.loop(0, turned.shape[0])
        def _(group):
            column = (2 * group + side) * out_rows if span == out_rows else group * span
            which = column // half
            base = jnp.where(which == core, OWN, PAIR)
            lanes = pl.ds(pl.multiple_of(column - which * half, 128), span)
            for block in range(2):
                turned[group, :, block * 2 * rows : (block + 1) * 2 * rows] = (
                    win[base + block, :, :, lanes].reshape(2 * rows, span).T
                )

    jobs = (
        lambda: couple(ACROSS, BACK_ACROSS),
        lambda: weigh(OWN, NEAR),
        lambda: weigh(NEAR, BACK_ACROSS),
        turn_over,
    )
    for index in range(PIECES):
        for job in jobs[index * len(jobs) // PIECES : (index + 1) * len(jobs) // PIECES]:
            job()
        arrive(4, index)
        send_route(5, index)
    couple(BACK_ACROSS, NEAR_ACROSS)
    for index in range(PIECES):
        arrive(3, index)
    couple(NEAR_ACROSS, FAR)
    weigh(BACK_ACROSS, NEAR_ACROSS)
    for index in range(PIECES):
        arrive(5, index)
    couple(FAR, FAR + 1)
    weigh(NEAR_ACROSS, FAR + 1)

    def w_copy(chunk):
        return remote(w.at[chunk, 0], w.at[chunk, 1], w_send.at[chunk], w_recv.at[chunk], across)

    for chunk in range(CHUNKS):
        w[chunk, 0] = acc[:, chunk * wide : (chunk + 1) * wide].astype(BF16)
        w_copy(chunk).start()
    def partial(chunk, group):
        return dot(turned[group], rr[chunk], ((1,), (0,)))

    def rows_of(target):
        return pl.multiple_of((2 * target + side) * out_rows, out_rows)

    def prepare(chunk):
        for block in range(2):
            if block:
                w_copy(chunk).wait_recv()
            top, low = w[chunk, block, :rows], w[chunk, block, rows:]
            first = 2 * rows * block
            rr[chunk, first : first + rows] = jnp.concatenate([top, low], axis=1)
            rr[chunk, first + rows : first + 2 * rows] = jnp.concatenate([low, -top], axis=1)

    def put(chunk, total, more=False):
        for part in range(2):
            for index in range(wide // 128):
                place = 2 * (chunk * wide // 128 + index) + part
                first = part * wide + index * 128
                value = total[:, first : first + 128]
                out_ref[:, place] = out_ref[:, place] + value if more else value

    def term(chunk, lane, slot, target, level_to):
        return remote(
            hp.at[chunk, pl.ds(rows_of(target), out_rows)], hr.at[chunk, lane, slot],
            h_send.at[chunk, target], h_recv.at[chunk, lane, slot], {"tile": 2 * level_to + side},
        )

    def onward(chunk, lane, target):
        return remote(
            hr.at[chunk, lane, target], hr.at[chunk, lane, target],
            o_send.at[chunk], h_recv.at[chunk, lane, target], {"tile": 2 * target + side},
        )

    if short_line(out_rows, levels):
        def flow(turn, first):
            lane = jnp.where(2 * level < levels, 1 - first, first)
            depth = jnp.where(lane == 0, level, levels - 1 - level)
            chunk = turn - jnp.maximum(depth - 1, 0)

            @pl.when((chunk >= 0) & (chunk < CHUNKS))
            def _():
                @pl.loop(0, levels - 1 - depth - jnp.where(depth == 0, 1, 0))
                def _(number):
                    target = jnp.where(lane == 0, levels - 1 - number, number)
                    total = partial(chunk, target)
                    passing = term(chunk, lane, target, target, level + 1 - 2 * lane)
                    place = pl.ds(rows_of(target), out_rows)

                    @pl.when(depth == 0)
                    def _():
                        hp[chunk, place] = total.astype(BF16)

                    @pl.when(depth == 1)
                    def _():
                        passing.wait_recv()
                        hp[chunk, place] = (total + hr[chunk, lane, target].astype(F32)).astype(BF16)

                    @pl.when(depth <= 1)
                    def _():
                        passing.start()

                    @pl.when(depth > 1)
                    def _():
                        passing.wait_recv()
                        onward(chunk, lane, target).start()
                        hp[chunk, place] = total.astype(BF16)
                        term(chunk, lane, levels, target, target).start()

        @pl.loop(0, CHUNKS + max(levels - 3, 0))
        def _(turn):
            @pl.when(turn < CHUNKS)
            def _():
                prepare(turn)

            flow(turn, 0)
            flow(turn, 1)

        @pl.when((level == 0) | (level == levels - 1))
        def _():
            lane = jnp.where(level == 0, 0, 1)
            target = level + 1 - 2 * lane

            @pl.loop(0, CHUNKS)
            def _(chunk):
                hp[chunk, pl.ds(rows_of(target), out_rows)] = partial(chunk, target).astype(BF16)
                term(chunk, lane, target, target, target).start()

        for chunk in range(CHUNKS):
            put(chunk, partial(chunk, level))
        for chunk in range(CHUNKS):
            before = level, levels - 1 - level
            for lane, slot, there in (
                (0, level, before[0] > 0), (1, level, before[1] > 0),
                (0, levels, before[0] > 2), (1, levels, before[1] > 2),
            ):
                @pl.when(there)
                def _(chunk=chunk, lane=lane, slot=slot):
                    term(chunk, lane, slot, level, level).wait_recv()
                    total = hr[chunk, lane, slot].astype(F32)
                    put(chunk, total, True)
    else:
        for chunk in range(CHUNKS):
            prepare(chunk)
            if span != out_rows:
                @pl.loop(0, hp.shape[1] // span)
                def _(group):
                    column = pl.multiple_of(group * span, span)
                    hp[chunk, pl.ds(column, span)] = partial(chunk, group).astype(BF16)

            @pl.loop(0, levels - 1)
            def _(number):
                target = other_level(number)
                if span == out_rows:
                    hp[chunk, pl.ds(rows_of(target), out_rows)] = partial(chunk, target).astype(BF16)
                term(chunk, 0, level, target, target).start()

            if span == out_rows:
                hp[chunk, pl.ds(rows_of(level), out_rows)] = partial(chunk, level).astype(BF16)

        for chunk in range(CHUNKS):
            def add(number, total):
                sender = other_level(number)
                term(chunk, 0, sender, level, sender).wait_recv()
                return total + hr[chunk, 0, sender].astype(F32)

            put(chunk, lax.fori_loop(0, levels - 1, add, hp[chunk, pl.ds(rows_of(level), out_rows)].astype(F32)))

    for number in range(len(ROUTES)):
        for index in range(PIECES):
            guarded(sends[number], lambda number=number, index=index: route(number, index).wait_send())
    to_pair(OWN, PAIR, 0).wait_send()
    to_pair(ACROSS, PAIR_ACROSS, 1).wait_send()
    image_copy.wait_send()

    @pl.loop(0, FAR + 1)
    def _(slot):
        @pl.when(exists(slot))
        def _():
            couple_copy(slot).wait_send()

    for chunk in range(CHUNKS):
        w_copy(chunk).wait_send()

        @pl.loop(0, levels - 1)
        def _(number):
            target = other_level(number)
            term(chunk, 0, target, target, target).wait_send()

        if short_line(out_rows, levels) and levels > 3:
            @pl.when((level == 2) | (levels - 1 - level == 2))
            def _(chunk=chunk):
                onward(chunk, 0, 0).wait_send()


def shards(count_tile, green, direction, partners, counts):
    tile_dev, kmax = partners.shape
    rows, half = green.shape[1:]
    sources = direction.shape[2]
    out_rows = sources // count_tile
    levels = count_tile // 2
    wide = half // CHUNKS
    lanes = 2 if short_line(out_rows, levels) else 1
    anywhere = pl.BlockSpec(memory_space=pl.ANY)
    local = pl.BlockSpec(memory_space=pltpu.VMEM)
    dma = pltpu.SemaphoreType.DMA
    out = pl.pallas_call(
        functools.partial(kernel, count_tile),
        out_shape=jax.ShapeDtypeStruct((out_rows, half // 64, 128), F32),
        in_specs=[anywhere] * 4,
        out_specs=local,
        scratch_shapes=[
            pltpu.SMEM((tile_dev, kmax), jnp.int32),
            pltpu.SMEM((tile_dev,), jnp.int32),
            pltpu.VMEM((9, 2, rows, half), BF16),
            pltpu.VMEM((2, 2, half, half), BF16),
            pltpu.VMEM((2 * rows, half), BF16),
            pltpu.VMEM((2, rows, half), F32),
            pltpu.VMEM((2, rows, half), F32),
            pltpu.VMEM((FAR + 1, 2, rows, rows), F32),
            pltpu.VMEM((FAR + 1, 2, rows, rows), F32),
            pltpu.VMEM((2 * rows, half), F32),
            pltpu.VMEM((CHUNKS, 2, 2 * rows, wide), BF16),
            pltpu.VMEM((levels if out_rows >= 128 else sources // 128, max(out_rows, 128), 4 * rows), BF16),
            pltpu.VMEM((CHUNKS, 4 * rows, 2 * wide), BF16),
            pltpu.VMEM((CHUNKS, sources, 2 * wide), BF16),
            pltpu.VMEM((CHUNKS, lanes, levels + 1, out_rows, 2 * wide), BF16),
            dma((5,)),
            dma((2,)),
            dma((len(ROUTES), PIECES)),
            dma((len(ROUTES), PIECES)),
            dma((FAR + 1,)),
            dma((FAR + 1,)),
            dma((2,)),
            dma((2,)),
            dma((CHUNKS,)),
            dma((CHUNKS,)),
            dma((CHUNKS, levels)),
            dma((CHUNKS, lanes, levels + 1)),
            dma((CHUNKS,)),
        ],
        compiler_params=pltpu.CompilerParams(
            collective_id=0, has_side_effects=True, vmem_limit_bytes=56 * 1024 * 1024
        ),
    )(green, direction, partners, counts)
    out = out.reshape(out_rows, half // 128, 2, 128)
    return jnp.swapaxes(out, 1, 2).reshape(out_rows, 2, half)


def solution(mesh):
    in_specs = (
        P(None, ("freq", "tile"), "src"),
        P(None, ("freq", "src"), None),
        P(("freq", "tile"), None),
        P(("freq", "tile")),
    )
    out_specs = P(("freq", "tile"), None, "src")
    body = functools.partial(shards, mesh.shape["tile"])
    return jax.shard_map(body, mesh=mesh, in_specs=in_specs, out_specs=out_specs, check_vma=False)
```
